32 devices in a mesh: tile: 8 (over z, x), col: 4 (over y, core).
Axes of the slice: x: 2, y: 2, z: 4, core: 2. Of those that a mesh axis runs over, the one named last changes fastest.
Arguments:
- readings: bfloat16 [64, 4, 512], P(('tile', 'col')), may hold values from -6 to 6
- sensitivity: bfloat16 [32768, 64, 64], P(('tile', 'col')), may hold values from -0.75 to 0.75
- kept_tile: int32 [32768], P(('tile', 'col')), may hold values from 0 to 7
- kept_row: int32 [32768], P(('tile', 'col')), may hold values from 0 to 7
- kept_slab: int32 [32768, 1], P(('tile', 'col')), may hold values from 0 to 31; in each aligned block of 1024 rows (0 to 1023, 1024 to 2047, ...) at most 80 rows name the same one
- kept_block: int32 [32768], P(('tile', 'col')), may hold values from 0 to 8191
Outputs:
- model_update: float32 [4, 256, 65536], P(None, None, ('tile', 'col'))
The draws below stay inside these ranges and needn't reach their ends.
Inputs may be any that keep to these rules, and one draw needn't show every extreme that they name: `kept_slab`: among the 1024 kept blocks held by one device, at most 80 name one slab, and in every draw some device has exactly 80 blocks naming one slab.
All inputs are finite; a program needn't handle non-finite values.
Results may differ from the reference program's by a relative error of at most 0.0029.
Values may be sent and summed in bfloat16 or wider, within the bound.
A program may use at most 128 MiB of HBM per device.

```python
import math
import jax
import jax.numpy as jnp
import numpy as np
from jax import lax

NX = 256
NY = 256
NZ = 256
VECS = 4
READINGS = 512
BLK = 64
LEVELS = 3
KEPT_DEV = 1024
TILES = 64
GROUP_TILES = 8
KEPT = 32768
CAP = 80
SLAB_BLOCKS = 8192
N_COL = 4
DEVICES = 32


def set_ends(entries, key, low, top_value):
    longest = entries.shape.index(max(entries.shape))
    spots = []
    for shift in (0, 1):
        where = [jax.random.randint(jax.random.fold_in(key, axis), (), 0, length) for axis, length in enumerate(entries.shape)]
        where[longest] = (where[longest] + shift) % entries.shape[longest]
        spots.append(tuple(where))
    return entries.at[spots[0]].set(low).at[spots[1]].set(top_value)


def shard_levels(stream_key, dims, shards, low, high):
    factor_of = 1.0
    for position, parts in shards:
        draws = jax.random.uniform(jax.random.fold_in(jax.random.fold_in(stream_key, 6), position), (parts,), jnp.float32, low / len(shards), high / len(shards))
        factor_of = factor_of * jnp.repeat(jnp.exp(draws), dims[position] // parts).reshape((-1,) + (1,) * (len(dims) - 1 - position))
    return factor_of


def routed_block(stream_key, own, number, rows, number_of, top, limit, skew):
    sequence = jax.random.permutation(stream_key, number_of)
    crowded, common = load_shares(number_of, rows * top, limit, skew, True), load_shares(number_of, rows * top, limit, skew, False)
    places = jnp.arange(number_of)

    def named(tallies, rotation):
        used = int((tallies > 0).sum())
        fixed = max(1, used // 4)
        passed = fixed + (places - fixed + rotation * (used - fixed)) % max(1, number_of - fixed)
        return jnp.zeros((number_of,), jnp.int32).at[sequence[jnp.where(places < fixed, places, passed)]].set(jnp.asarray(tallies, jnp.int32))

    tallies = jnp.where(number % 4 == 0, named(crowded, number // 4), named(common, number - number // 4 - 1))
    mixed = jax.random.permutation(jax.random.fold_in(own, 3), number_of)
    giver, receiver = mixed[0:number_of // 2 * 2:2], mixed[1:number_of // 2 * 2:2]
    margin = jnp.minimum(tallies[giver] - 1, limit - tallies[receiver]) // 2
    margin = jnp.where((giver == sequence[0]) | (receiver == sequence[0]) | (tallies[receiver] == 0), 0, jnp.maximum(margin, 0))
    passed = jax.random.randint(jax.random.fold_in(own, 4), (number_of // 2,), 0, 1 << 20) % (margin + 1)
    tallies = tallies.at[giver].add(-passed).at[receiver].add(passed)
    labels = jnp.searchsorted(jnp.cumsum(tallies), jnp.arange(rows * top), side="right").astype(jnp.int32)
    grid = labels.reshape(top, rows).T
    grid = grid[jax.random.permutation(jax.random.fold_in(own, 1), rows)]
    rotation = jax.random.randint(jax.random.fold_in(own, 2), (rows, 1), 0, top)
    return jnp.take_along_axis(grid, (jnp.arange(top)[None, :] + rotation) % top, axis=1)


def load_shares(number_of, total, reach, skew, full):
    loads = [(1 << 20) // math.isqrt(standing ** skew) + 1 for standing in range(1, number_of + 1)]
    largest = reach if full else min(reach, max(-(-total // number_of), total * loads[0] // sum(loads)))
    least = 1 if total - largest >= number_of - 1 else 0
    holding, spare = [largest] + [least] * (number_of - 1), total - largest - least * (number_of - 1)
    while spare > 0:
        free = [i for i in range(1, number_of) if holding[i] < largest] or [i for i in range(1, number_of) if holding[i] < reach]
        mass, budget = sum([loads[i] for i in free]), spare
        for i in free:
            extra = min(reach - holding[i], max(1, budget * loads[i] // mass), spare)
            holding[i] = holding[i] + extra
            spare = spare - extra
    return np.array(holding)


def bell_draw(stream_key, shape, scale, limit, split=(), kind=jnp.bfloat16):
    values = scale * jax.random.normal(stream_key, shape, jnp.float32)
    if split:
        values = values * shard_levels(stream_key, shape, split, -0.22, 0.18)
    return jnp.clip(values, -limit, limit).astype(kind)


def setup_inputs(seed: int = 0) -> dict:
    splits = jax.random.split(jax.random.key(seed), 7)
    readings = bell_draw(splits[0], (TILES, VECS, READINGS), 1.0, 6.0, ((0, 32),))
    sensitivity = bell_draw(splits[1], (KEPT, BLK, BLK), BLK ** -0.5, 0.75, ((0, 32),))
    kept_tile = set_ends(jax.random.randint(splits[2], (KEPT,), 0, GROUP_TILES), jax.random.fold_in(splits[2], 1), 0, GROUP_TILES - 1).astype(jnp.int32)
    kept_row = set_ends(jax.random.randint(splits[3], (KEPT,), 0, READINGS // BLK), jax.random.fold_in(splits[3], 1), 0, (READINGS // BLK) - 1).astype(jnp.int32)
    kept_slab_keys = jax.random.split(jax.random.fold_in(splits[4], 1), KEPT // KEPT_DEV)
    kept_slab_turns = jax.random.permutation(jax.random.fold_in(splits[4], 3), KEPT // KEPT_DEV)
    kept_slab = jax.vmap(lambda own, number: routed_block(jax.random.fold_in(splits[4], 2), own, number, KEPT_DEV, DEVICES, 1, CAP, 2))(kept_slab_keys, kept_slab_turns).reshape((KEPT, 1))
    kept_block = set_ends(jax.random.randint(splits[5], (KEPT,), 0, SLAB_BLOCKS), jax.random.fold_in(splits[5], 1), 0, SLAB_BLOCKS - 1).astype(jnp.int32)
    return {"readings": readings, "sensitivity": sensitivity, "kept_tile": kept_tile, "kept_row": kept_row, "kept_slab": kept_slab, "kept_block": kept_block}


def inverse_haar(values, dimension):
    length = values.shape[dimension]
    span_now = length // (2 ** LEVELS)
    coarse_part = lax.slice_in_dim(values, 0, span_now, axis=dimension)
    for level in range(LEVELS):
        detail = lax.slice_in_dim(values, span_now, 2 * span_now, axis=dimension)
        even_part = (coarse_part + detail) * 0.7071067811865476
        odd_part = (coarse_part - detail) * 0.7071067811865476
        paired = jnp.stack([even_part, odd_part], axis=dimension + 1)
        new_shape = list(coarse_part.shape)
        new_shape[dimension] = 2 * span_now
        coarse_part = paired.reshape(new_shape)
        span_now = 2 * span_now
    return coarse_part


def reference(readings, sensitivity, kept_tile, kept_row, kept_slab, kept_block):
    total = sensitivity.shape[0]
    group_rows = KEPT_DEV * N_COL
    tile_ids = (jnp.arange(total, dtype=jnp.int32) // group_rows) * GROUP_TILES + kept_tile
    split_readings = readings.reshape(TILES, VECS, READINGS // BLK, BLK)
    row_step = 8192

    def contribute(pieces):
        sens_part, tiles_part, rows_part = pieces
        picked = split_readings[tiles_part, :, rows_part]
        product = jnp.einsum("krj,kvr->kvj", sens_part.astype(jnp.float32), picked.astype(jnp.float32))
        return product.astype(jnp.bfloat16)

    contrib = lax.map(contribute, (sensitivity.reshape(-1, row_step, BLK, BLK), tile_ids.reshape(-1, row_step), kept_row.reshape(-1, row_step)))
    contrib = contrib.reshape(total, VECS * BLK)
    block_ids = kept_slab[:, 0] * SLAB_BLOCKS + kept_block
    coef = jnp.zeros((NZ * NX * (NY // BLK), VECS * BLK), jnp.float32).at[block_ids].add(contrib.astype(jnp.float32))
    coef = coef.reshape(NZ, NX, NY // BLK, VECS, BLK).transpose(3, 0, 2, 4, 1).reshape(VECS, NZ, NY, NX)
    plane = inverse_haar(inverse_haar(coef, 2), 3)
    return inverse_haar(plane, 1).reshape(VECS, NZ, NY * NX)
```

```python
import functools

import jax
import jax.numpy as jnp
from jax import lax
from jax.experimental import pallas as pl
from jax.experimental.pallas import tpu as pltpu
from jax.sharding import PartitionSpec as P

NX = 256
NY = 256
NZ = 256
LEVELS = 3
ROOT = 0.7071067811865476
LANES = 128
BUCKET = 8
STEP = 8
AXES = ("tile", "col")


def segments(length):
    coarse = length // 2**LEVELS
    found = [(0, coarse, 2**LEVELS)]
    for level in range(LEVELS):
        found.append((coarse * 2**level, coarse * 2**level, 2 ** (LEVELS - level)))
    return found


def haar_sign(out_index, in_index, length):
    value = jnp.zeros(jnp.broadcast_shapes(out_index.shape, in_index.shape), jnp.float32)
    for number, (start, count, reach) in enumerate(segments(length)):
        inside = (in_index >= start) & (in_index < start + count)
        meets = inside & (out_index // reach == in_index - start)
        sign = jnp.where(out_index % reach < reach // 2, 1.0, -1.0) if number else 1.0
        value = jnp.where(meets, sign, value)
    return value


def haar_scale(in_index, length):
    scale = jnp.zeros(in_index.shape, jnp.float32)
    for start, count, reach in segments(length):
        inside = (in_index >= start) & (in_index < start + count)
        scale = jnp.where(inside, ROOT ** (reach.bit_length() - 1), scale)
    return scale


def y_plan(y_share, width):
    rows = []
    used = {}
    for start, count, reach in segments(NY):
        group = min(start // width, 2)
        for i in range(max(1, y_share // reach)):
            slot = used.get(group, 0)
            used[group] = slot + 1
            rows.append((start, reach, i, slot, group))
    return rows, max(used.values())


def contrib_kernel(ids_ref, table_ref, sens_ref, out_ref):
    rows = ids_ref.shape[0]
    count, width, _ = sens_ref.shape
    vectors = rows // count
    wide = table_ref.shape[1]
    pack = wide // width
    spots = lax.broadcasted_iota(jnp.int32, (rows, table_ref.shape[0]), 1)
    chosen = jnp.where(ids_ref[...] == spots, 1.0, 0.0).astype(jnp.bfloat16)
    picked = jnp.dot(chosen, table_ref[...], preferred_element_type=jnp.float32)
    row = lax.broadcasted_iota(jnp.int32, (rows, wide), 0)
    lane = lax.broadcasted_iota(jnp.int32, (rows, wide), 1)
    own = (row // vectors) % pack == lane // width
    left = jnp.where(own, picked, 0.0).astype(jnp.bfloat16)
    sens = sens_ref[...].reshape(count * width, width)
    step = pack * vectors
    for g in range(count // pack):
        out_ref[g * step : (g + 1) * step, :] = jnp.dot(
            left[g * step : (g + 1) * step, :],
            sens[g * wide : (g + 1) * wide, :],
            preferred_element_type=jnp.float32,
        ).astype(jnp.bfloat16)


def two_part_dot(a, b, split_left):
    whole = a if split_left else b
    high = whole.astype(jnp.bfloat16)
    low = (whole - high.astype(jnp.float32)).astype(jnp.bfloat16)
    if split_left:
        pair = jnp.dot(high, b, preferred_element_type=jnp.float32)
        return pair + jnp.dot(low, b, preferred_element_type=jnp.float32)
    pair = jnp.dot(a, high, preferred_element_type=jnp.float32)
    return pair + jnp.dot(a, low, preferred_element_type=jnp.float32)


def model_kernel(
    plan, vectors, off_ref, vals_ref, ids_ref, hy_ref, hx_ref, hz_ref, scale_ref, out_ref, plane, left, right, total
):
    sources = vals_ref.shape[0]
    slots = vals_ref.shape[1] // vectors
    buckets = NZ // BUCKET
    y_share = hy_ref.shape[0] // (vectors * BUCKET)
    per_y = NY // 64

    def clear(i, carry):
        right[:, pl.ds(pl.multiple_of(i * LANES, LANES), LANES)] = jnp.zeros((NX, LANES), jnp.bfloat16)
        return carry

    lax.fori_loop(0, right.shape[1] // LANES, clear, 0)

    def bucket_step(s, carry):
        layer = lax.broadcasted_iota(jnp.int32, (BUCKET, LANES), 0) + s * BUCKET
        across = lax.broadcasted_iota(jnp.int32, (NX, LANES), 0)

        def chunk(src, block, used):
            base = pl.multiple_of(block * LANES, LANES)
            ids = ids_ref[src, :, pl.ds(base, LANES)]
            vals = vals_ref[src, :, pl.ds(base, LANES)].astype(jnp.float32)
            depth = ids // (NX * per_y)
            x = (ids // per_y) % NX
            b = jnp.minimum(ids % per_y, 2)
            there = depth == layer
            marks = [jnp.where(there & (b == g), 1.0, 0.0) for g in range(3)]
            pieces = []
            for _, _, _, slot, group in plan:
                for v in range(vectors):
                    line = vals[v * slots + slot : v * slots + slot + 1, :]
                    pieces.append(line * marks[group])
            place = pl.ds(pl.multiple_of(used * LANES, LANES), LANES)
            left[:, place] = jnp.concatenate(pieces, axis=0).astype(jnp.bfloat16)
            right[:, place] = jnp.where(x == across, 1.0, 0.0).astype(jnp.bfloat16)
            return used + 1

        def source_step(src, used):
            at = src * (buckets + 1) + s
            low = off_ref[at]
            high = off_ref[at + 1]
            first = low // LANES
            last = jnp.where(high > low, (high + LANES - 1) // LANES, first)
            return lax.fori_loop(first, last, lambda block, n: chunk(src, block, n), used)

        used = lax.fori_loop(0, sources, source_step, 0)
        rounds = (used + STEP - 1) // STEP

        def pad(i, carry):
            left[:, pl.ds(pl.multiple_of(i * LANES, LANES), LANES)] = jnp.zeros((left.shape[0], LANES), jnp.bfloat16)
            return carry

        lax.fori_loop(used, rounds * STEP, pad, 0)
        total[...] = jnp.zeros_like(total)

        def add(i, carry):
            place = pl.ds(pl.multiple_of(i * STEP * LANES, LANES), STEP * LANES)
            total[...] += lax.dot_general(
                left[:, place], right[:, place], (((1,), (1,)), ((), ())), preferred_element_type=jnp.float32
            )
            return carry

        lax.fori_loop(0, rounds, add, 0)
        z = s * BUCKET
        depth_scale = jnp.float32(0.0)
        for start, count, reach in segments(NZ):
            inside = (z >= start) & (z < start + count)
            depth_scale = jnp.where(inside, jnp.float32(ROOT ** (reach.bit_length() - 1)), depth_scale)
        coef = total[...] * (scale_ref[...] * depth_scale)
        along_y = two_part_dot(hy_ref[...], coef, False)
        along_x = two_part_dot(along_y, hx_ref[...], True)
        rows = pl.ds(pl.multiple_of(z, BUCKET), BUCKET)
        for y in range(y_share):
            for v in range(vectors):
                at = (y * vectors + v) * BUCKET
                plane[v, rows, y * NX : (y + 1) * NX] = along_x[at : at + BUCKET, :]
        return carry

    lax.fori_loop(0, buckets, bucket_step, 0)

    def finish(v, carry):
        for y in range(y_share):
            part = plane[v, :, y * NX : (y + 1) * NX]
            out_ref[v, :, y * NX : (y + 1) * NX] = two_part_dot(hz_ref[...], part, False)
        return carry

    lax.fori_loop(0, vectors, finish, 0)


def on_device(readings, sensitivity, kept_tile, kept_row, kept_slab, kept_block):
    devices = lax.axis_size(AXES)
    columns = lax.axis_size("col")
    me = lax.axis_index(AXES)
    kept, width, _ = sensitivity.shape
    vectors = readings.shape[1]
    per_y = NY // width
    layers = NZ // devices
    y_share = NY // devices
    buckets = NZ // BUCKET
    plan, slots = y_plan(y_share, width)

    depth = kept_slab[:, 0] * layers + kept_block // (NX * per_y)
    spot = depth * (NX * per_y) + kept_block % (NX * per_y)
    number = jnp.arange(kept, dtype=jnp.int32)
    key = (depth // BUCKET) * kept + number
    position = jnp.sum((key[None, :] < key[:, None]).astype(jnp.int32), axis=1)
    moved = position[:, None] == number[None, :]
    spots = jnp.sum(jnp.where(moved, spot[:, None], 0), axis=0)
    all_spots = lax.all_to_all(
        jnp.broadcast_to(spots[None], (devices, kept)), AXES, split_axis=0, concat_axis=0, tiled=True
    )
    group = lax.all_to_all(
        jnp.broadcast_to(readings[None], (columns, *readings.shape)), "col", split_axis=0, concat_axis=0, tiled=True
    )
    row_blocks = readings.shape[2] // width
    table = jnp.tile(group.reshape(-1, width), (1, 256 // width))
    ids = (kept_tile[:, None] * vectors + jnp.arange(vectors, dtype=jnp.int32)[None, :]) * row_blocks + kept_row[:, None]
    chunk = 64
    contrib = pl.pallas_call(
        contrib_kernel,
        out_shape=jax.ShapeDtypeStruct((kept * vectors, width), jnp.bfloat16),
        grid=(kept // chunk,),
        in_specs=[
            pl.BlockSpec((chunk * vectors, 1), lambda i: (i, 0)),
            pl.BlockSpec(table.shape, lambda i: (0, 0)),
            pl.BlockSpec((chunk, width, width), lambda i: (i, 0, 0)),
        ],
        out_specs=pl.BlockSpec((chunk * vectors, width), lambda i: (i, 0)),
    )(ids.reshape(kept * vectors, 1), table, sensitivity)
    contrib = contrib.reshape(kept, vectors * width)

    in_y = spot % per_y
    masked = jnp.concatenate([jnp.where((in_y == b)[:, None], contrib, 0) for b in range(per_y)], axis=1)
    row = jnp.arange(per_y * vectors * width, dtype=jnp.int32)[:, None]
    lane = jnp.arange(devices * vectors * slots, dtype=jnp.int32)[None, :]
    y_of_row = row // (vectors * width) * width + row % width
    owner = lane // (vectors * slots)
    spread = jnp.zeros((row.shape[0], lane.shape[1]), jnp.bool_)
    for start, reach, i, slot, _ in plan:
        spread = spread | ((lane % slots == slot) & (y_of_row == start + (owner * y_share) // reach + i))
    spread = spread & (row // width % vectors == lane // slots % vectors)
    sorted_by = jnp.dot(masked, spread.astype(jnp.bfloat16), preferred_element_type=jnp.float32).astype(jnp.bfloat16)
    outgoing = lax.dot_general(
        sorted_by, moved.astype(jnp.bfloat16), (((0,), (0,)), ((), ())), preferred_element_type=jnp.float32
    ).astype(jnp.bfloat16)
    arrived = lax.all_to_all(
        outgoing.reshape(devices, vectors * slots, kept), AXES, split_axis=0, concat_axis=0, tiled=True
    )

    edges = jnp.arange(buckets + 1, dtype=jnp.int32) * (BUCKET * NX * per_y)
    offsets = jnp.sum((all_spots[:, None, :] < edges[None, :, None]).astype(jnp.int32), axis=2).reshape(-1)
    full = jnp.arange(NX, dtype=jnp.int32)
    sign_x = haar_sign(full[None, :], full[:, None], NX).astype(jnp.bfloat16)
    sign_z = haar_sign(full[:, None], full[None, :], NZ).astype(jnp.bfloat16)
    inner = vectors * BUCKET
    needs = jnp.stack([start + (me * y_share) // reach + i for start, reach, i, _, _ in plan]).astype(jnp.int32)
    needs = jnp.repeat(needs, inner)
    line = jnp.arange(y_share * inner, dtype=jnp.int32)
    same = line[:, None] % inner == jnp.arange(len(plan) * inner, dtype=jnp.int32)[None, :] % inner
    sign_y = haar_sign(me * y_share + line[:, None] // inner, needs[None, :], NY)
    sign_y = jnp.where(same, sign_y, 0.0).astype(jnp.bfloat16)
    scale = haar_scale(needs, NY)[:, None] * haar_scale(full, NX)[None, :]
    reach = -(-(2 * devices) // STEP) * STEP * LANES
    vmem = pl.BlockSpec(memory_space=pltpu.VMEM)
    return pl.pallas_call(
        functools.partial(model_kernel, plan, vectors),
        out_shape=jax.ShapeDtypeStruct((vectors, NZ, y_share * NX), jnp.float32),
        in_specs=[pl.BlockSpec(memory_space=pltpu.SMEM)] + [vmem] * 6,
        out_specs=vmem,
        scratch_shapes=[
            pltpu.VMEM((vectors, NZ, y_share * NX), jnp.float32),
            pltpu.VMEM((len(plan) * inner, reach), jnp.bfloat16),
            pltpu.VMEM((NX, reach), jnp.bfloat16),
            pltpu.VMEM((len(plan) * inner, NX), jnp.float32),
        ],
        compiler_params=pltpu.CompilerParams(vmem_limit_bytes=60 * 2**20),
    )(offsets, arrived, all_spots[:, None, :], sign_y, sign_x, sign_z, scale)


def solution(mesh):
    return jax.shard_map(
        on_device,
        mesh=mesh,
        in_specs=(
            P(AXES, None, None),
            P(AXES, None, None),
            P(AXES),
            P(AXES),
            P(AXES, None),
            P(AXES),
        ),
        out_specs=P(None, None, AXES),
        check_vma=False,
    )
```

```python
import functools

import jax
import jax.numpy as jnp
from jax import lax
from jax.experimental import pallas as pl
from jax.experimental.pallas import tpu as pltpu
from jax.sharding import PartitionSpec as P

NX = 256
NY = 256
NZ = 256
LEVELS = 3
ROOT = 0.7071067811865476
LANES = 128
BUCKET = 8
MOVES = 8
ROUND = 512
AXES = ("tile", "col")


def segments(length):
    coarse = length // 2**LEVELS
    found = [(0, coarse, 2**LEVELS)]
    for level in range(LEVELS):
        found.append((coarse * 2**level, coarse * 2**level, 2 ** (LEVELS - level)))
    return found


def haar_sign(out_index, in_index, length):
    value = jnp.zeros(jnp.broadcast_shapes(out_index.shape, in_index.shape), jnp.float32)
    for number, (start, count, reach) in enumerate(segments(length)):
        inside = (in_index >= start) & (in_index < start + count)
        meets = inside & (out_index // reach == in_index - start)
        sign = jnp.where(out_index % reach < reach // 2, 1.0, -1.0) if number else 1.0
        value = jnp.where(meets, sign, value)
    return value


def haar_scale(in_index, length):
    scale = jnp.zeros(in_index.shape, jnp.float32)
    for start, count, reach in segments(length):
        inside = (in_index >= start) & (in_index < start + count)
        scale = jnp.where(inside, ROOT ** (reach.bit_length() - 1), scale)
    return scale


def y_plan(y_share, width):
    rows = []
    used = {}
    for start, count, reach in segments(NY):
        group = min(start // width, 2)
        for i in range(max(1, y_share // reach)):
            slot = used.get(group, 0)
            used[group] = slot + 1
            rows.append((start, reach, i, slot, group))
    return rows, max(used.values())


def contrib_kernel(ids_ref, table_ref, sens_ref, out_ref):
    width, columns, lanes = sens_ref.shape
    vectors = table_ref.shape[0] // width
    spots = lax.broadcasted_iota(jnp.int32, (table_ref.shape[1], lanes), 0)
    chosen = jnp.where(ids_ref[...] == spots, 1.0, 0.0).astype(jnp.bfloat16)
    picked = jnp.dot(table_ref[...], chosen, preferred_element_type=jnp.float32)
    sums = [jnp.zeros((columns, lanes), jnp.float32) for _ in range(vectors)]
    for r in range(width):
        sens = sens_ref[r].astype(jnp.float32)
        for v in range(vectors):
            sums[v] = sums[v] + sens * picked[v * width + r : v * width + r + 1, :]
    for v in range(vectors):
        out_ref[v * columns : (v + 1) * columns, :] = sums[v].astype(jnp.bfloat16)


def two_part_dot(a, b, split_left):
    whole = a if split_left else b
    high = whole.astype(jnp.bfloat16)
    low = (whole - high.astype(jnp.float32)).astype(jnp.bfloat16)
    if split_left:
        pair = jnp.dot(high, b, preferred_element_type=jnp.float32)
        return pair + jnp.dot(low, b, preferred_element_type=jnp.float32)
    pair = jnp.dot(a, high, preferred_element_type=jnp.float32)
    return pair + jnp.dot(a, low, preferred_element_type=jnp.float32)


def model_kernel(
    plan, vectors, off_ref, to_ref, start_ref, vals_ref, ids_ref, hy_ref, hx_ref, hz_ref, scale_ref, out_ref,
    plane, vals_in, ids_in, left, right, total
):
    sources = vals_ref.shape[0]
    kept = vals_ref.shape[2]
    slots = vals_ref.shape[1] // vectors
    buckets = NZ // BUCKET
    y_share = hy_ref.shape[0] // (vectors * BUCKET)
    per_y = NY // 64
    y_bits = per_y.bit_length() - 1
    x_bits = NX.bit_length() - 1
    window = 2 * LANES

    def clear(i, carry):
        place = pl.ds(pl.multiple_of(i * window, LANES), window)
        ids_in[:, place] = jnp.full((BUCKET, window), -1, jnp.int32)
        vals_in[:, place] = jnp.zeros((vals_in.shape[0], window), jnp.float32)
        return carry

    lax.fori_loop(0, ids_in.shape[1] // window, clear, 0)
    lane = lax.broadcasted_iota(jnp.int32, (BUCKET, window), 1)
    lanes_all = lax.broadcasted_iota(jnp.int32, (vals_in.shape[0], window), 1)

    def move(step, carry):
        s = step // (sources // MOVES)
        for u in range(MOVES):
            src = (step % (sources // MOVES)) * MOVES + u
            low = off_ref[src * (buckets + 1) + s]
            high = off_ref[src * (buckets + 1) + s + 1]
            to = to_ref[src * buckets + s]
            base = jnp.minimum((low // LANES) * LANES, kept - window)
            begin = to % LANES
            shift = (begin - (low - base) + 2 * window) % window
            place = pl.ds(pl.multiple_of(base, LANES), window)
            target = pl.ds(pl.multiple_of((to // LANES) * LANES, LANES), window)
            ids = jnp.broadcast_to(ids_ref[src, :, place], (BUCKET, window))
            vals = vals_ref[src, :, place].astype(jnp.float32)
            ids = pltpu.roll(ids, shift, 1)
            vals = pltpu.roll(vals, shift, 1)
            end = begin + high - low
            ids_in[:, target] = jnp.where((lane >= begin) & (lane < end), ids, ids_in[:, target])
            vals_in[:, target] = jnp.where((lanes_all >= begin) & (lanes_all < end), vals, vals_in[:, target])
        return carry

    lax.fori_loop(0, buckets * (sources // MOVES), move, 0)

    def bucket_step(s, carry):
        layer = lax.broadcasted_iota(jnp.int32, (BUCKET, ROUND), 0) + s * BUCKET
        row = lax.broadcasted_iota(jnp.int32, (BUCKET, ROUND), 0)
        first = start_ref[s]
        total[...] = jnp.zeros_like(total)

        def add(i, carry):
            place = pl.ds(pl.multiple_of(first + i * ROUND, LANES), ROUND)
            ids = ids_in[:, place]
            vals = vals_in[:, place]
            x = (ids >> y_bits) & (NX - 1)
            b = jnp.minimum(ids & (per_y - 1), 2)
            there = (ids >> (y_bits + x_bits)) == layer
            marks = [jnp.where(there & (b == g), 1.0, 0.0) for g in range(3)]
            pieces = []
            for _, _, _, slot, group in plan:
                for v in range(vectors):
                    line = vals[v * slots + slot : v * slots + slot + 1, :]
                    pieces.append(line * marks[group])
            left[...] = jnp.concatenate(pieces, axis=0).astype(jnp.bfloat16)
            hits = [jnp.where(x - row == n, 1.0, 0.0) for n in range(0, NX, BUCKET)]
            right[...] = jnp.concatenate(hits, axis=0).astype(jnp.bfloat16)
            total[...] += lax.dot_general(
                left[...], right[...], (((1,), (1,)), ((), ())), preferred_element_type=jnp.float32
            )
            return carry

        lax.fori_loop(0, (start_ref[s + 1] - first) // ROUND, add, 0)
        z = s * BUCKET
        depth_scale = jnp.float32(0.0)
        for start, count, reach in segments(NZ):
            inside = (z >= start) & (z < start + count)
            depth_scale = jnp.where(inside, jnp.float32(ROOT ** (reach.bit_length() - 1)), depth_scale)
        coef = total[...] * (scale_ref[...] * depth_scale)
        along_y = two_part_dot(hy_ref[...], coef, False)
        along_x = two_part_dot(along_y, hx_ref[...], True)
        rows = pl.ds(pl.multiple_of(z, BUCKET), BUCKET)
        for y in range(y_share):
            for v in range(vectors):
                at = (y * vectors + v) * BUCKET
                plane[v, rows, y * NX : (y + 1) * NX] = along_x[at : at + BUCKET, :]
        return carry

    lax.fori_loop(0, buckets, bucket_step, 0)

    def finish(v, carry):
        for y in range(y_share):
            part = plane[v, :, y * NX : (y + 1) * NX]
            out_ref[v, :, y * NX : (y + 1) * NX] = two_part_dot(hz_ref[...], part, False)
        return carry

    lax.fori_loop(0, vectors, finish, 0)


def on_device(readings, sensitivity, kept_tile, kept_row, kept_slab, kept_block):
    devices = lax.axis_size(AXES)
    columns = lax.axis_size("col")
    me = lax.axis_index(AXES)
    kept, width, _ = sensitivity.shape
    vectors = readings.shape[1]
    per_y = NY // width
    layers = NZ // devices
    y_share = NY // devices
    buckets = NZ // BUCKET
    plan, slots = y_plan(y_share, width)

    depth = kept_slab[:, 0] * layers + kept_block // (NX * per_y)
    spot = depth * (NX * per_y) + kept_block % (NX * per_y)
    number = jnp.arange(kept, dtype=jnp.int32)
    key = (depth // BUCKET) * kept + number
    position = jnp.sum((key[None, :] < key[:, None]).astype(jnp.int32), axis=1)
    moved = position[:, None] == number[None, :]
    spots = jnp.sum(jnp.where(moved, spot[:, None], 0), axis=0)
    all_spots = lax.all_to_all(
        jnp.broadcast_to(spots[None], (devices, kept)), AXES, split_axis=0, concat_axis=0, tiled=True
    )
    group = lax.all_to_all(
        jnp.broadcast_to(readings[None], (columns, *readings.shape)), "col", split_axis=0, concat_axis=0, tiled=True
    )
    row_blocks = readings.shape[2] // width
    table = group.reshape(-1, vectors, row_blocks, width).transpose(1, 3, 0, 2).reshape(vectors * width, -1)
    ids = (kept_tile * row_blocks + kept_row)[None, :]
    contrib = pl.pallas_call(
        contrib_kernel,
        out_shape=jax.ShapeDtypeStruct((vectors * width, kept), jnp.bfloat16),
        grid=(kept // LANES,),
        in_specs=[
            pl.BlockSpec((1, LANES), lambda i: (0, i)),
            pl.BlockSpec(table.shape, lambda i: (0, 0)),
            pl.BlockSpec((width, width, LANES), lambda i: (0, 0, i)),
        ],
        out_specs=pl.BlockSpec((vectors * width, LANES), lambda i: (0, i)),
    )(ids, table, sensitivity.transpose(1, 2, 0))

    in_y = spot % per_y
    masked = jnp.concatenate([jnp.where((in_y == b)[None, :], contrib, 0) for b in range(per_y)], axis=0)
    row = jnp.arange(per_y * vectors * width, dtype=jnp.int32)[None, :]
    lane = jnp.arange(devices * vectors * slots, dtype=jnp.int32)[:, None]
    y_of_row = row // (vectors * width) * width + row % width
    owner = lane // (vectors * slots)
    spread = jnp.zeros((lane.shape[0], row.shape[1]), jnp.bool_)
    for start, reach, i, slot, _ in plan:
        spread = spread | ((lane % slots == slot) & (y_of_row == start + (owner * y_share) // reach + i))
    spread = spread & (row // width % vectors == lane // slots % vectors)
    chosen = jnp.dot(spread.astype(jnp.bfloat16), masked, preferred_element_type=jnp.float32).astype(jnp.bfloat16)
    outgoing = jnp.dot(chosen, moved.astype(jnp.bfloat16), preferred_element_type=jnp.float32).astype(jnp.bfloat16)
    arrived = lax.all_to_all(
        outgoing.reshape(devices, vectors * slots, kept), AXES, split_axis=0, concat_axis=0, tiled=True
    )

    edges = jnp.arange(buckets + 1, dtype=jnp.int32) * (BUCKET * NX * per_y)
    offsets = jnp.sum((all_spots[:, None, :] < edges[None, :, None]).astype(jnp.int32), axis=2)
    counts = offsets[:, 1:] - offsets[:, :-1]
    source = jnp.arange(devices, dtype=jnp.int32)
    ahead = jnp.sum(jnp.where(source[:, None, None] > source[None, :, None], counts[None], 0), axis=1)
    rounds = (jnp.sum(counts, axis=0) + ROUND - 1) // ROUND
    bucket = jnp.arange(buckets + 1, dtype=jnp.int32)
    starts = jnp.sum(jnp.where(bucket[:, None] > bucket[None, :-1], rounds[None, :], 0), axis=1) * ROUND
    to = ahead + starts[None, :-1]
    full = jnp.arange(NX, dtype=jnp.int32)
    sign_x = haar_sign(full[None, :], full[:, None], NX).astype(jnp.bfloat16)
    sign_z = haar_sign(full[:, None], full[None, :], NZ).astype(jnp.bfloat16)
    inner = vectors * BUCKET
    needs = jnp.stack([start + (me * y_share) // reach + i for start, reach, i, _, _ in plan]).astype(jnp.int32)
    needs = jnp.repeat(needs, inner)
    line = jnp.arange(y_share * inner, dtype=jnp.int32)
    same = line[:, None] % inner == jnp.arange(len(plan) * inner, dtype=jnp.int32)[None, :] % inner
    sign_y = haar_sign(me * y_share + line[:, None] // inner, needs[None, :], NY)
    sign_y = jnp.where(same, sign_y, 0.0).astype(jnp.bfloat16)
    scale = haar_scale(needs, NY)[:, None] * haar_scale(full, NX)[None, :]
    room = devices * kept + buckets * ROUND + 2 * LANES
    vmem = pl.BlockSpec(memory_space=pltpu.VMEM)
    smem = pl.BlockSpec(memory_space=pltpu.SMEM)
    return pl.pallas_call(
        functools.partial(model_kernel, plan, vectors),
        out_shape=jax.ShapeDtypeStruct((vectors, NZ, y_share * NX), jnp.float32),
        in_specs=[smem] * 3 + [vmem] * 6,
        out_specs=vmem,
        scratch_shapes=[
            pltpu.VMEM((vectors, NZ, y_share * NX), jnp.float32),
            pltpu.VMEM((vectors * slots, room), jnp.float32),
            pltpu.VMEM((BUCKET, room), jnp.int32),
            pltpu.VMEM((len(plan) * inner, ROUND), jnp.bfloat16),
            pltpu.VMEM((NX, ROUND), jnp.bfloat16),
            pltpu.VMEM((len(plan) * inner, NX), jnp.float32),
        ],
        compiler_params=pltpu.CompilerParams(vmem_limit_bytes=60 * 2**20),
    )(offsets.reshape(-1), to.reshape(-1), starts, arrived, all_spots[:, None, :], sign_y, sign_x, sign_z, scale)


def solution(mesh):
    return jax.shard_map(
        on_device,
        mesh=mesh,
        in_specs=(
            P(AXES, None, None),
            P(AXES, None, None),
            P(AXES),
            P(AXES),
            P(AXES, None),
            P(AXES),
        ),
        out_specs=P(None, None, AXES),
        check_vma=False,
    )
```

```python
import functools

import jax
import jax.numpy as jnp
from jax import lax
from jax.experimental import pallas as pl
from jax.experimental.pallas import tpu as pltpu
from jax.sharding import PartitionSpec as P

NX = 256
NY = 256
NZ = 256
LEVELS = 3
ROOT = 0.7071067811865476
LANES = 128
BUCKET = 8
MOVES = 16
ROUND = 512
AXES = ("tile", "col")


def segments(length):
    coarse = length // 2**LEVELS
    found = [(0, coarse, 2**LEVELS)]
    for level in range(LEVELS):
        found.append((coarse * 2**level, coarse * 2**level, 2 ** (LEVELS - level)))
    return found


def haar_sign(out_index, in_index, length):
    value = jnp.zeros(jnp.broadcast_shapes(out_index.shape, in_index.shape), jnp.float32)
    for number, (start, count, reach) in enumerate(segments(length)):
        inside = (in_index >= start) & (in_index < start + count)
        meets = inside & (out_index // reach == in_index - start)
        sign = jnp.where(out_index % reach < reach // 2, 1.0, -1.0) if number else 1.0
        value = jnp.where(meets, sign, value)
    return value


def haar_scale(in_index, length):
    scale = jnp.zeros(in_index.shape, jnp.float32)
    for start, count, reach in segments(length):
        inside = (in_index >= start) & (in_index < start + count)
        scale = jnp.where(inside, ROOT ** (reach.bit_length() - 1), scale)
    return scale


def y_plan(y_share, width):
    rows = []
    used = {}
    for start, count, reach in segments(NY):
        group = min(start // width, 2)
        for i in range(max(1, y_share // reach)):
            slot = used.get(group, 0)
            used[group] = slot + 1
            rows.append((start, reach, i, slot, group))
    return rows, max(used.values())


def contrib_kernel(ids_ref, table_ref, sens_ref, out_ref):
    width, columns, lanes = sens_ref.shape
    vectors = table_ref.shape[0] // width
    spots = lax.broadcasted_iota(jnp.int32, (table_ref.shape[1], lanes), 0)
    chosen = jnp.where(ids_ref[...] == spots, 1.0, 0.0).astype(jnp.bfloat16)
    picked = jnp.dot(table_ref[...], chosen, preferred_element_type=jnp.float32)
    sums = [jnp.zeros((columns, lanes), jnp.float32) for _ in range(vectors)]
    for r in range(width):
        sens = sens_ref[r].astype(jnp.float32)
        for v in range(vectors):
            sums[v] = sums[v] + sens * picked[v * width + r : v * width + r + 1, :]
    for v in range(vectors):
        out_ref[v * columns : (v + 1) * columns, :] = sums[v].astype(jnp.bfloat16)


def two_part_dot(a, b, split_left):
    whole = a if split_left else b
    high = whole.astype(jnp.bfloat16)
    low = (whole - high.astype(jnp.float32)).astype(jnp.bfloat16)
    if split_left:
        pair = jnp.dot(high, b, preferred_element_type=jnp.float32)
        return pair + jnp.dot(low, b, preferred_element_type=jnp.float32)
    pair = jnp.dot(a, high, preferred_element_type=jnp.float32)
    return pair + jnp.dot(a, low, preferred_element_type=jnp.float32)


def model_kernel(
    plan, vectors, off_ref, to_ref, start_ref, vals_ref, ids_ref, hy_ref, hx_ref, hz_ref, scale_ref, out_ref,
    plane, vals_in, ids_in, left, right, total
):
    sources = vals_ref.shape[0]
    kept = vals_ref.shape[2]
    slots = vals_ref.shape[1] // vectors
    buckets = NZ // BUCKET
    y_share = hy_ref.shape[0] // (vectors * BUCKET)
    per_y = NY // 64
    y_bits = per_y.bit_length() - 1
    x_bits = NX.bit_length() - 1
    window = 2 * LANES

    def clear(i, carry):
        place = pl.ds(pl.multiple_of(i * window, LANES), window)
        ids_in[:, place] = jnp.full((BUCKET, window), -1, jnp.int32)
        vals_in[:, place] = jnp.zeros((vals_in.shape[0], window), jnp.float32)
        return carry

    lax.fori_loop(0, ids_in.shape[1] // window, clear, 0)
    lane = lax.broadcasted_iota(jnp.int32, (BUCKET, window), 1)
    lanes_all = lax.broadcasted_iota(jnp.int32, (vals_in.shape[0], window), 1)

    def move(step, carry):
        s = step // (sources // MOVES)
        for u in range(MOVES):
            src = (step % (sources // MOVES)) * MOVES + u
            low = off_ref[src * (buckets + 1) + s]
            high = off_ref[src * (buckets + 1) + s + 1]
            to = to_ref[src * buckets + s]
            base = jnp.minimum((low // LANES) * LANES, kept - window)
            begin = to % LANES
            shift = (begin - (low - base) + 2 * window) % window
            place = pl.ds(pl.multiple_of(base, LANES), window)
            target = pl.ds(pl.multiple_of((to // LANES) * LANES, LANES), window)
            ids = jnp.broadcast_to(ids_ref[src, :, place], (BUCKET, window))
            vals = vals_ref[src, :, place].astype(jnp.float32)
            ids = pltpu.roll(ids, shift, 1)
            vals = pltpu.roll(vals, shift, 1)
            end = begin + high - low
            ids_in[:, target] = jnp.where((lane >= begin) & (lane < end), ids, ids_in[:, target])
            vals_in[:, target] = jnp.where((lanes_all >= begin) & (lanes_all < end), vals, vals_in[:, target])
        return carry

    lax.fori_loop(0, buckets * (sources // MOVES), move, 0)

    def bucket_step(s, carry):
        layer = lax.broadcasted_iota(jnp.int32, (BUCKET, ROUND), 0) + s * BUCKET
        row = lax.broadcasted_iota(jnp.int32, (BUCKET, ROUND), 0)
        first = start_ref[s]
        total[...] = jnp.zeros_like(total)

        def add(i, carry):
            place = pl.ds(pl.multiple_of(first + i * ROUND, LANES), ROUND)
            ids = ids_in[:, place]
            vals = vals_in[:, place]
            x = (ids >> y_bits) & (NX - 1)
            b = jnp.minimum(ids & (per_y - 1), 2)
            there = (ids >> (y_bits + x_bits)) == layer
            marks = [jnp.where(there & (b == g), 1.0, 0.0) for g in range(3)]
            pieces = []
            for _, _, _, slot, group in plan:
                for v in range(vectors):
                    line = vals[v * slots + slot : v * slots + slot + 1, :]
                    pieces.append(line * marks[group])
            left[...] = jnp.concatenate(pieces, axis=0).astype(jnp.bfloat16)
            hits = [jnp.where(x - row == n, 1.0, 0.0) for n in range(0, NX, BUCKET)]
            right[...] = jnp.concatenate(hits, axis=0).astype(jnp.bfloat16)
            total[...] += lax.dot_general(
                left[...], right[...], (((1,), (1,)), ((), ())), preferred_element_type=jnp.float32
            )
            return carry

        lax.fori_loop(0, (start_ref[s + 1] - first) // ROUND, add, 0)
        z = s * BUCKET
        depth_scale = jnp.float32(0.0)
        for start, count, reach in segments(NZ):
            inside = (z >= start) & (z < start + count)
            depth_scale = jnp.where(inside, jnp.float32(ROOT ** (reach.bit_length() - 1)), depth_scale)
        coef = total[...] * (scale_ref[...] * depth_scale)
        along_y = two_part_dot(hy_ref[...], coef, False)
        along_x = two_part_dot(along_y, hx_ref[...], True)
        rows = pl.ds(pl.multiple_of(z, BUCKET), BUCKET)
        for y in range(y_share):
            for v in range(vectors):
                at = (y * vectors + v) * BUCKET
                plane[v, rows, y * NX : (y + 1) * NX] = along_x[at : at + BUCKET, :]
        return carry

    lax.fori_loop(0, buckets, bucket_step, 0)

    def finish(v, carry):
        for y in range(y_share):
            part = plane[v, :, y * NX : (y + 1) * NX].astype(jnp.bfloat16)
            out_ref[v, :, y * NX : (y + 1) * NX] = jnp.dot(hz_ref[...], part, preferred_element_type=jnp.float32)
        return carry

    lax.fori_loop(0, vectors, finish, 0)


def on_device(readings, sensitivity, kept_tile, kept_row, kept_slab, kept_block):
    devices = lax.axis_size(AXES)
    columns = lax.axis_size("col")
    me = lax.axis_index(AXES)
    kept, width, _ = sensitivity.shape
    vectors = readings.shape[1]
    per_y = NY // width
    layers = NZ // devices
    y_share = NY // devices
    buckets = NZ // BUCKET
    plan, slots = y_plan(y_share, width)

    depth = kept_slab[:, 0] * layers + kept_block // (NX * per_y)
    spot = depth * (NX * per_y) + kept_block % (NX * per_y)
    number = jnp.arange(kept, dtype=jnp.int32)
    key = (depth // BUCKET) * kept + number
    position = jnp.sum((key[None, :] < key[:, None]).astype(jnp.int32), axis=1)
    moved = position[:, None] == number[None, :]
    spots = jnp.sum(jnp.where(moved, spot[:, None], 0), axis=0)
    all_spots = lax.all_to_all(
        jnp.broadcast_to(spots[None], (devices, kept)), AXES, split_axis=0, concat_axis=0, tiled=True
    )
    group = lax.all_to_all(
        jnp.broadcast_to(readings[None], (columns, *readings.shape)), "col", split_axis=0, concat_axis=0, tiled=True
    )
    row_blocks = readings.shape[2] // width
    table = group.reshape(-1, vectors, row_blocks, width).transpose(1, 3, 0, 2).reshape(vectors * width, -1)
    ids = (kept_tile * row_blocks + kept_row)[None, :]
    contrib = pl.pallas_call(
        contrib_kernel,
        out_shape=jax.ShapeDtypeStruct((vectors * width, kept), jnp.bfloat16),
        grid=(kept // LANES,),
        in_specs=[
            pl.BlockSpec((1, LANES), lambda i: (0, i)),
            pl.BlockSpec(table.shape, lambda i: (0, 0)),
            pl.BlockSpec((width, width, LANES), lambda i: (0, 0, i)),
        ],
        out_specs=pl.BlockSpec((vectors * width, LANES), lambda i: (0, i)),
    )(ids, table, sensitivity.transpose(1, 2, 0))

    contrib = jnp.dot(contrib, moved.astype(jnp.bfloat16), preferred_element_type=jnp.float32).astype(jnp.bfloat16)
    in_y = spots % per_y
    masked = jnp.concatenate([jnp.where((in_y == b)[None, :], contrib, 0) for b in range(per_y)], axis=0)
    row = jnp.arange(per_y * vectors * width, dtype=jnp.int32)[None, :]
    lane = jnp.arange(devices * vectors * slots, dtype=jnp.int32)[:, None]
    y_of_row = row // (vectors * width) * width + row % width
    owner = lane // (vectors * slots)
    spread = jnp.zeros((lane.shape[0], row.shape[1]), jnp.bool_)
    for start, reach, i, slot, _ in plan:
        spread = spread | ((lane % slots == slot) & (y_of_row == start + (owner * y_share) // reach + i))
    spread = spread & (row // width % vectors == lane // slots % vectors)
    outgoing = jnp.dot(spread.astype(jnp.bfloat16), masked, preferred_element_type=jnp.float32).astype(jnp.bfloat16)
    arrived = lax.all_to_all(
        outgoing.reshape(devices, vectors * slots, kept), AXES, split_axis=0, concat_axis=0, tiled=True
    )

    edges = jnp.arange(buckets + 1, dtype=jnp.int32) * (BUCKET * NX * per_y)
    offsets = jnp.sum((all_spots[:, None, :] < edges[None, :, None]).astype(jnp.int32), axis=2)
    counts = offsets[:, 1:] - offsets[:, :-1]
    source = jnp.arange(devices, dtype=jnp.int32)
    ahead = jnp.sum(jnp.where(source[:, None, None] > source[None, :, None], counts[None], 0), axis=1)
    rounds = (jnp.sum(counts, axis=0) + ROUND - 1) // ROUND
    bucket = jnp.arange(buckets + 1, dtype=jnp.int32)
    starts = jnp.sum(jnp.where(bucket[:, None] > bucket[None, :-1], rounds[None, :], 0), axis=1) * ROUND
    to = ahead + starts[None, :-1]
    full = jnp.arange(NX, dtype=jnp.int32)
    sign_x = haar_sign(full[None, :], full[:, None], NX).astype(jnp.bfloat16)
    sign_z = haar_sign(full[:, None], full[None, :], NZ).astype(jnp.bfloat16)
    inner = vectors * BUCKET
    needs = jnp.stack([start + (me * y_share) // reach + i for start, reach, i, _, _ in plan]).astype(jnp.int32)
    needs = jnp.repeat(needs, inner)
    line = jnp.arange(y_share * inner, dtype=jnp.int32)
    same = line[:, None] % inner == jnp.arange(len(plan) * inner, dtype=jnp.int32)[None, :] % inner
    sign_y = haar_sign(me * y_share + line[:, None] // inner, needs[None, :], NY)
    sign_y = jnp.where(same, sign_y, 0.0).astype(jnp.bfloat16)
    scale = haar_scale(needs, NY)[:, None] * haar_scale(full, NX)[None, :]
    room = devices * kept + buckets * ROUND + 2 * LANES
    vmem = pl.BlockSpec(memory_space=pltpu.VMEM)
    smem = pl.BlockSpec(memory_space=pltpu.SMEM)
    return pl.pallas_call(
        functools.partial(model_kernel, plan, vectors),
        out_shape=jax.ShapeDtypeStruct((vectors, NZ, y_share * NX), jnp.float32),
        in_specs=[smem] * 3 + [vmem] * 6,
        out_specs=vmem,
        scratch_shapes=[
            pltpu.VMEM((vectors, NZ, y_share * NX), jnp.float32),
            pltpu.VMEM((vectors * slots, room), jnp.float32),
            pltpu.VMEM((BUCKET, room), jnp.int32),
            pltpu.VMEM((len(plan) * inner, ROUND), jnp.bfloat16),
            pltpu.VMEM((NX, ROUND), jnp.bfloat16),
            pltpu.VMEM((len(plan) * inner, NX), jnp.float32),
        ],
        compiler_params=pltpu.CompilerParams(vmem_limit_bytes=60 * 2**20),
    )(offsets.reshape(-1), to.reshape(-1), starts, arrived, all_spots[:, None, :], sign_y, sign_x, sign_z, scale)


def solution(mesh):
    return jax.shard_map(
        on_device,
        mesh=mesh,
        in_specs=(
            P(AXES, None, None),
            P(AXES, None, None),
            P(AXES),
            P(AXES),
            P(AXES, None),
            P(AXES),
        ),
        out_specs=P(None, None, AXES),
        check_vma=False,
    )
```
